32 devices in a mesh: sa: 16 (over z, x, core), sb: 2 (over y).
Axes of the slice: x: 2, y: 2, z: 4, core: 2. Of those that a mesh axis runs over, the one named last changes fastest.
Arguments:
- tokens: bfloat16 [64, 32, 32, 2048], P('sa', 'sb'), may hold values from -6 to 6
- norm_gain: float32 [2048], replicated, may hold values from 0.5 to 1.5
- gate_weight: bfloat16 [2048, 2048], P(('sa', 'sb')), may hold values from -0.125 to 0.125
- level_one: bfloat16 [32, 32, 64, 64], P('sb', 'sa'), may hold values from -0.75 to 0.75
- level_two: bfloat16 [64, 32, 32, 32], P('sa', 'sb'), may hold values from -1 to 1
- level_three: bfloat16 [64, 32, 32, 32], P('sa', 'sb'), may hold values from -1 to 1
- upstream: bfloat16 [64, 32, 32, 2048], P('sa', 'sb'), may hold values from -6 to 6
Outputs:
- output: bfloat16 [64, 32, 32, 2048], P('sa', 'sb')
- grad_tokens: bfloat16 [64, 32, 32, 2048], P('sa', 'sb')
- grad_one: float32 [32, 32, 64, 64], P('sb', 'sa')
- grad_two: float32 [64, 32, 32, 32], P('sa', 'sb')
- grad_three: float32 [64, 32, 32, 32], P('sa', 'sb')
The draws below stay inside these ranges and needn't reach their ends.
All inputs are finite; a program needn't handle non-finite values.
Results may differ from the reference program's by a relative error of at most 0.0071.
Values may be sent and summed in bfloat16 or wider, within the bound.
No kernel may reach another device: no remote copies, remote signals or barrier semaphores. Data moves between devices by JAX's collectives and lax.ppermute only.
A program may use at most 192 MiB of HBM per device.

```python
import math
import jax
import jax.numpy as jnp
from jax import lax

D = 2048
M1 = 64
M2 = 32
M3 = 32


def level_of(own_key, extent, pieces, low, largest):
    loudness, own = 1.0, jax.random.fold_in(own_key, 6)
    for dim, shards_of in pieces:
        steps = jnp.exp(jax.random.uniform(jax.random.fold_in(own, dim), (shards_of,), jnp.float32, low / len(pieces), largest / len(pieces)))
        loudness = loudness * jnp.repeat(steps, extent[dim] // shards_of).reshape([-1 if axis == dim else 1 for axis in range(len(extent))])
    return loudness


def noise(key, dims, scale, most, pieces=(), held_as=jnp.bfloat16):
    drawn = scale * jax.random.normal(key, dims, jnp.float32)
    if pieces:
        drawn = drawn * level_of(key, dims, pieces, -0.22, 0.18)
    return jnp.clip(drawn, -most, most).astype(held_as)


def setup_inputs(seed: int = 0) -> dict:
    streams_of = jax.random.split(jax.random.key(seed), 8)
    return {
        "tokens": noise(streams_of[0], (M1, M2, M3, D), 1.0, 6.0, ((0, 16), (1, 2))),
        "norm_gain": jnp.clip(1.0 + 0.1 * jax.random.normal(streams_of[1], (D,), jnp.float32), 0.5, 1.5),
        "gate_weight": noise(streams_of[2], (D, D), D ** -0.5, 0.125, ((0, 32),)),
        "level_one": noise(streams_of[3], (M2, M3, M1, M1), M1 ** -0.5, 0.75, ((0, 2), (1, 16))),
        "level_two": noise(streams_of[4], (M1, M3, M2, M2), M2 ** -0.5, 1.0, ((0, 16), (1, 2))),
        "level_three": noise(streams_of[5], (M1, M2, M3, M3), M3 ** -0.5, 1.0, ((0, 16), (1, 2))),
        "upstream": noise(streams_of[6], (M1, M2, M3, D), 1.0, 6.0, ((0, 16), (1, 2))),
    }


EPSILON = 1e-06

def blend_levels(pattern, weights, values):
    return jnp.einsum(pattern, weights.astype(jnp.float32), values.astype(jnp.float32))

def reference(tokens, norm_gain, gate_weight, level_one, level_two, level_three, upstream):
    tokens_float = tokens.astype(jnp.float32)
    inverse_rms = lax.rsqrt(lax.optimization_barrier(jnp.mean(tokens_float * tokens_float, axis=3, keepdims=True)) + EPSILON)
    normed = (tokens_float * inverse_rms * norm_gain).astype(jnp.bfloat16)
    token_rows = normed.reshape(-1, D)
    block_width = math.gcd(D, 128)
    block_count = D // block_width

    def block_terms(totals, block_index):
        back_total, total_one, total_two, total_three = totals
        offset = block_index * block_width
        columns = lax.dynamic_slice_in_dim(gate_weight, offset, block_width, 1)
        gate_pre = jnp.dot(token_rows, columns, preferred_element_type=jnp.float32).reshape(M1, M2, M3, block_width)
        normed_part = lax.dynamic_slice_in_dim(normed, offset, block_width, 3)
        first_mix = blend_levels('jkoi,ijkc->ojkc', level_one, normed_part).astype(jnp.bfloat16)
        second_mix = blend_levels('ikoj,ijkc->iokc', level_two, first_mix).astype(jnp.bfloat16)
        mixed_all = blend_levels('ijok,ijkc->ijoc', level_three, second_mix)
        gate_sigmoid = jax.nn.sigmoid(gate_pre)
        gate_value = gate_pre * gate_sigmoid
        token_part = lax.dynamic_slice_in_dim(tokens_float, offset, block_width, 3)
        output_part = (token_part + mixed_all * gate_value).astype(jnp.bfloat16)
        upstream_part = lax.dynamic_slice_in_dim(upstream, offset, block_width, 3).astype(jnp.float32)
        grad_mixed = (upstream_part * gate_value).astype(jnp.bfloat16)
        grad_gate = (upstream_part * mixed_all * gate_sigmoid * (1.0 + gate_pre * (1.0 - gate_sigmoid))).astype(jnp.bfloat16)
        total_three = total_three + blend_levels('ijoc,ijkc->ijok', grad_mixed, second_mix)
        grad_second = blend_levels('ijok,ijoc->ijkc', level_three, grad_mixed).astype(jnp.bfloat16)
        total_two = total_two + blend_levels('iokc,ijkc->ikoj', grad_second, first_mix)
        grad_first = blend_levels('ikoj,iokc->ijkc', level_two, grad_second).astype(jnp.bfloat16)
        total_one = total_one + blend_levels('ojkc,ijkc->jkoi', grad_first, normed_part)
        grad_normed = blend_levels('jkoi,ojkc->ijkc', level_one, grad_first).astype(jnp.bfloat16)
        back_total = back_total + jnp.dot(grad_gate.reshape(-1, block_width), columns.T, preferred_element_type=jnp.float32)
        return ((back_total, total_one, total_two, total_three), (output_part, grad_normed))
    start_totals = (jnp.zeros((M1 * M2 * M3, D), jnp.float32), jnp.zeros((M2, M3, M1, M1), jnp.float32), jnp.zeros((M1, M3, M2, M2), jnp.float32), jnp.zeros((M1, M2, M3, M3), jnp.float32))
    totals, stacked = lax.scan(block_terms, start_totals, jnp.arange(block_count, dtype=jnp.int32))
    back_total, total_one, total_two, total_three = totals
    output = jnp.moveaxis(stacked[0], 0, 3).reshape(M1, M2, M3, D)
    grad_normed = jnp.moveaxis(stacked[1], 0, 3).reshape(M1, M2, M3, D)
    grad_hidden = grad_normed.astype(jnp.float32) + back_total.reshape(M1, M2, M3, D)
    weighted = grad_hidden * norm_gain
    average = lax.optimization_barrier(jnp.mean(weighted * tokens_float, axis=3, keepdims=True))
    grad_tokens = (upstream.astype(jnp.float32) + inverse_rms * weighted - tokens_float * inverse_rms ** 3 * average).astype(jnp.bfloat16)
    grad_scale = D ** (-0.5)
    return (output, grad_tokens, total_one * grad_scale, total_two * grad_scale, total_three * grad_scale)
```

```python
import functools

import jax
import jax.numpy as jnp
from jax import lax
from jax.experimental import pallas as pl
from jax.experimental.pallas import tpu as pltpu
from jax.sharding import PartitionSpec as P

EPSILON = 1e-06
F32 = jnp.float32
BF16 = jnp.bfloat16
CHUNKS = 4
LIMIT = 60 * 1024 * 1024


def dot(left, right):
    return jnp.dot(left, right, preferred_element_type=F32)


def dot_last(left, right):
    return lax.dot_general(left, right, (((1,), (1,)), ((), ())), preferred_element_type=F32)


def position(shape, axis, inner, extent):
    return (lax.broadcasted_iota(jnp.int32, shape, axis) // inner) % extent


def widen(rows, inner, extent, lanes):
    batch, count, width = rows.shape
    wide = width * extent
    source = lax.broadcasted_iota(jnp.int32, (width, wide), 0)
    column = lax.broadcasted_iota(jnp.int32, (width, wide), 1)
    pick = (source == (column // (extent * lanes)) * lanes + column % lanes).astype(BF16)
    full = jnp.einsum("brq,qw->brw", rows, pick, preferred_element_type=F32)
    keep = position((count, wide), 0, inner, extent) == position((count, wide), 1, lanes, extent)
    return jnp.where(keep[None], full, 0.0).astype(BF16)


def fold(total, inner, extent, lanes):
    count, wide = total.shape
    width = wide // extent
    keep = position((count, wide), 0, inner, extent) == position((count, wide), 1, lanes, extent)
    source = lax.broadcasted_iota(jnp.int32, (wide, width), 1)
    column = lax.broadcasted_iota(jnp.int32, (wide, width), 0)
    pick = (source == (column // (extent * lanes)) * lanes + column % lanes).astype(F32)
    return jnp.dot(
        jnp.where(keep, total, 0.0), pick, precision=lax.Precision.HIGHEST, preferred_element_type=F32
    )


def params(count):
    return pltpu.CompilerParams(
        dimension_semantics=("arbitrary",) * count, vmem_limit_bytes=LIMIT
    )


def cost(flops, moved):
    return pl.CostEstimate(flops=int(flops), bytes_accessed=int(moved), transcendentals=0)


def first_kernel(matrix, values, out):
    shape = out.shape
    flat = values[...].reshape(-1, shape[3])
    out[...] = dot(matrix[0], flat).astype(BF16).reshape(shape)


def first_level(matrix, values):
    away, low, rows, width = values.shape
    if rows % 16:
        flat = values.transpose(1, 0, 2, 3).reshape(low, away * rows, width)
        mixed = jnp.einsum("krs,ksc->krc", matrix, flat, preferred_element_type=F32).astype(BF16)
        return mixed.reshape(low, away, rows, width).transpose(1, 0, 2, 3)
    size = away * rows
    spec = pl.BlockSpec((away, 1, rows, width), lambda k: (0, k, 0, 0))
    return pl.pallas_call(
        first_kernel,
        grid=(low,),
        in_specs=[pl.BlockSpec((1, size, size), lambda k: (k, 0, 0)), spec],
        out_specs=spec,
        out_shape=jax.ShapeDtypeStruct(values.shape, BF16),
        compiler_params=params(1),
        cost_estimate=cost(2 * low * size * size * width, 4 * values.size + 2 * matrix.size),
        name="first",
    )(matrix, values)


def first_back_kernel(lanes, matrix, values, grads, out, total):
    shape = out.shape
    flat = values[...].reshape(-1, shape[3])
    grad = grads[...].reshape(-1, shape[3])
    out[...] = dot(matrix[0], grad).astype(BF16).reshape(shape)
    total[0] = fold(dot_last(grad, flat), 1, lanes, 1)


def first_back(matrix, values, grads, lanes):
    away, low, rows, width = values.shape
    size = away * rows
    if rows % 16:
        flat = values.transpose(1, 0, 2, 3).reshape(low, size, width)
        grad = grads.transpose(1, 0, 2, 3).reshape(low, size, width)
        mixed = jnp.einsum("krs,ksc->krc", matrix, grad, preferred_element_type=F32).astype(BF16)
        full = jnp.einsum("krc,ksc->krs", grad, flat, preferred_element_type=F32)
        total = jnp.stack([fold(full[k], 1, lanes, 1) for k in range(low)])
        return (mixed.reshape(low, away, rows, width).transpose(1, 0, 2, 3), total)
    spec = pl.BlockSpec((away, 1, rows, width), lambda k: (0, k, 0, 0))
    return pl.pallas_call(
        functools.partial(first_back_kernel, lanes),
        grid=(low,),
        in_specs=[pl.BlockSpec((1, size, size), lambda k: (k, 0, 0)), spec, spec],
        out_specs=(spec, pl.BlockSpec((1, size, size // lanes), lambda k: (k, 0, 0))),
        out_shape=(
            jax.ShapeDtypeStruct(values.shape, BF16),
            jax.ShapeDtypeStruct((low, size, size // lanes), F32),
        ),
        compiler_params=params(1),
        cost_estimate=cost(4 * low * size * size * width, 6 * values.size + 2 * matrix.size),
        name="first_back",
    )(matrix, values, grads)


def second_kernel(parts, matrix, *refs):
    ins, outs = refs[:parts], refs[parts:]
    rows = outs[0].shape[1]
    for k in range(matrix.shape[0]):
        flat = jnp.concatenate([ref[k] for ref in ins], axis=0)
        mixed = dot(matrix[k], flat).astype(BF16)
        for part in range(parts):
            outs[part][k] = mixed[part * rows : (part + 1) * rows]


def second_level(matrix, pieces):
    parts = len(pieces)
    count, rows, width = pieces[0].shape
    if rows % 16:
        flat = jnp.concatenate(pieces, axis=1)
        mixed = jnp.einsum("krs,ksc->krc", matrix, flat, preferred_element_type=F32).astype(BF16)
        return tuple(jnp.split(mixed, parts, axis=1))
    step = 4 if count % 4 == 0 else 1
    size = parts * rows
    spec = pl.BlockSpec((step, rows, width), lambda k: (k, 0, 0))
    return pl.pallas_call(
        functools.partial(second_kernel, parts),
        grid=(count // step,),
        in_specs=[pl.BlockSpec((step, size, size), lambda k: (k, 0, 0))] + [spec] * parts,
        out_specs=(spec,) * parts,
        out_shape=(jax.ShapeDtypeStruct(pieces[0].shape, BF16),) * parts,
        compiler_params=params(1),
        cost_estimate=cost(2 * count * size * size * width, 4 * parts * pieces[0].size),
        name="second",
    )(matrix, *pieces)


def second_back_kernel(parts, inner, lanes, matrix, *refs):
    grads, values = refs[:parts], refs[parts : 2 * parts]
    outs, total = refs[2 * parts : 3 * parts], refs[3 * parts]
    rows = outs[0].shape[1]
    for k in range(matrix.shape[0]):
        grad = jnp.concatenate([ref[k] for ref in grads], axis=0)
        flat = jnp.concatenate([ref[k] for ref in values], axis=0)
        mixed = dot(matrix[k], grad).astype(BF16)
        for part in range(parts):
            outs[part][k] = mixed[part * rows : (part + 1) * rows]
        total[k] = fold(dot_last(grad, flat), inner, lanes, inner)


def second_back(matrix, grads, values, inner, lanes):
    parts = len(grads)
    count, rows, width = grads[0].shape
    size = parts * rows
    if rows % 16:
        grad = jnp.concatenate(grads, axis=1)
        flat = jnp.concatenate(values, axis=1)
        mixed = jnp.einsum("krs,ksc->krc", matrix, grad, preferred_element_type=F32).astype(BF16)
        full = jnp.einsum("krc,ksc->krs", grad, flat, preferred_element_type=F32)
        total = jnp.stack([fold(full[k], inner, lanes, inner) for k in range(count)])
        return (tuple(jnp.split(mixed, parts, axis=1)), total)
    step = 4 if count % 4 == 0 else 1
    spec = pl.BlockSpec((step, rows, width), lambda k: (k, 0, 0))
    result = pl.pallas_call(
        functools.partial(second_back_kernel, parts, inner, lanes),
        grid=(count // step,),
        in_specs=[pl.BlockSpec((step, size, size), lambda k: (k, 0, 0))] + [spec] * (2 * parts),
        out_specs=(spec,) * parts
        + (pl.BlockSpec((step, size, size // lanes), lambda k: (k, 0, 0)),),
        out_shape=(jax.ShapeDtypeStruct(grads[0].shape, BF16),) * parts
        + (jax.ShapeDtypeStruct((count, size, size // lanes), F32),),
        compiler_params=params(1),
        cost_estimate=cost(4 * count * size * size * width, 6 * parts * grads[0].size),
        name="second_back",
    )(matrix, *grads, *values)
    return (result[:parts], result[parts])


def gate_math(mixed, gate_pre, tokens, upstream):
    gate_sigmoid = jax.nn.sigmoid(gate_pre)
    gate_value = gate_pre * gate_sigmoid
    output = (tokens.astype(F32) + mixed * gate_value).astype(BF16)
    upstream = upstream.astype(F32)
    grad_mixed = (upstream * gate_value).astype(BF16)
    grad_gate = (
        upstream * mixed * gate_sigmoid * (1.0 + gate_pre * (1.0 - gate_sigmoid))
    ).astype(BF16)
    return (output, grad_mixed, grad_gate)


def third_kernel(parts, lanes, matrix, matrix_back, gate_pre, tokens, upstream, *refs):
    ins = refs[:parts]
    output, grad_gate = refs[parts], refs[parts + 1]
    outs, total = refs[parts + 2 : 2 * parts + 2], refs[2 * parts + 2]
    shape = output.shape
    width = shape[3]
    flat = jnp.concatenate([ref[...].reshape(-1, width) for ref in ins], axis=0)
    mixed = dot(matrix[0], flat)
    result, grad_mixed, gate_grad = gate_math(
        mixed,
        gate_pre[...].reshape(-1, width),
        tokens[...].reshape(-1, width),
        upstream[...].reshape(-1, width),
    )
    output[...] = result.reshape(shape)
    grad_gate[...] = gate_grad.reshape(shape)
    back = dot(matrix_back[0], grad_mixed).astype(BF16)
    rows = back.shape[0] // parts
    for part in range(parts):
        outs[part][...] = back[part * rows : (part + 1) * rows].reshape(outs[part].shape)
    total[0] = fold(dot_last(grad_mixed, flat), 1, lanes, 1)


def third_level(matrix, matrix_back, gate_pre, tokens, upstream, offset, pieces):
    parts = len(pieces)
    low, heads, lanes, width = pieces[0].shape
    count = low * parts
    size = count * lanes
    if lanes % 16:
        flat = jnp.concatenate(pieces, axis=0).transpose(1, 0, 2, 3).reshape(heads, size, width)
        mixed = jnp.einsum("irs,isc->irc", matrix, flat, preferred_element_type=F32)

        def turn(value):
            return value.reshape(heads, count, lanes, width).transpose(1, 0, 2, 3)

        def local(value):
            value = lax.slice_in_dim(value, offset * width, (offset + 1) * width, axis=3)
            return value.transpose(1, 0, 2, 3).reshape(heads, size, width)

        pre = gate_pre.transpose(1, 0, 2, 3).reshape(heads, size, width)
        result, grad_mixed, gate_grad = gate_math(mixed, pre, local(tokens), local(upstream))
        back = jnp.einsum("irs,isc->irc", matrix_back, grad_mixed, preferred_element_type=F32)
        full = jnp.einsum("irc,isc->irs", grad_mixed, flat, preferred_element_type=F32)
        total = jnp.stack([fold(full[i], 1, lanes, 1) for i in range(heads)])
        outs = tuple(jnp.split(turn(back.astype(BF16)), parts, axis=0))
        return (turn(result), turn(gate_grad), outs, total)
    whole = pl.BlockSpec((count, 1, lanes, width), lambda i: (0, i, 0, 0))
    shifted = pl.BlockSpec((count, 1, lanes, width), lambda i: (0, i, 0, offset))
    part = pl.BlockSpec((low, 1, lanes, width), lambda i: (0, i, 0, 0))
    square = pl.BlockSpec((1, size, size), lambda i: (i, 0, 0))
    full = jax.ShapeDtypeStruct((count, heads, lanes, width), BF16)
    result = pl.pallas_call(
        functools.partial(third_kernel, parts, lanes),
        grid=(heads,),
        in_specs=[square, square, whole, shifted, shifted] + [part] * parts,
        out_specs=(whole, whole)
        + (part,) * parts
        + (pl.BlockSpec((1, size, count), lambda i: (i, 0, 0)),),
        out_shape=(full, full)
        + (jax.ShapeDtypeStruct(pieces[0].shape, BF16),) * parts
        + (jax.ShapeDtypeStruct((heads, size, count), F32),),
        compiler_params=params(1),
        cost_estimate=cost(6 * heads * size * size * width, 18 * heads * size * width),
        name="third",
    )(matrix, matrix_back, gate_pre, tokens, upstream, *pieces)
    return (result[0], result[1], result[2 : parts + 2], result[parts + 2])


def ahead(values, axis, me, count):
    doubled = jnp.concatenate([values, values], axis=axis)
    return lax.dynamic_slice_in_dim(doubled, me, count, axis=axis)


def behind(values, axis, me, count):
    return ahead(jnp.flip(values, axis=axis), axis, count - 1 - me, count)


def exchange(blocks):
    count = len(blocks)
    return [blocks[0]] + [
        lax.ppermute(blocks[r], "sb", [(n, (n + r) % count) for n in range(count)])
        for r in range(1, count)
    ]


def across_first(values):
    return lax.all_to_all(values, "sa", split_axis=0, concat_axis=0, tiled=True)


def body(parts, away, tokens, norm_gain, gate_weight, level_one, level_two, level_three, upstream):
    heads, lanes, thirds, channels = tokens.shape
    firsts = level_one.shape[2]
    low = thirds // away
    near = thirds // parts
    me = lax.axis_index("sb")
    width = channels // CHUNKS
    rows = heads * lanes

    tokens_float = tokens.astype(F32)
    inverse_rms = lax.rsqrt(jnp.mean(tokens_float * tokens_float, axis=3, keepdims=True) + EPSILON)

    def normalised(values, scale, gain):
        return (values.astype(F32) * scale * gain).astype(BF16)

    spreads = []
    for n in range(CHUNKS):
        at = slice(n * width, (n + 1) * width)
        part = normalised(tokens[..., at], inverse_rms, norm_gain[at])
        part = part.transpose(2, 0, 1, 3).reshape(away, low, rows, width)
        spreads.append(across_first(part))

    weight = lax.all_gather(gate_weight, ("sa", "sb"), axis=0, tiled=True)
    one = level_one.transpose(1, 2, 0, 3).reshape(low, firsts * lanes, firsts)
    one_back = level_one.transpose(1, 3, 0, 2).reshape(low, firsts * lanes, firsts)
    matrix_one = widen(one, 1, lanes, 1)
    matrix_one_back = widen(one_back, 1, lanes, 1)

    two = level_two.reshape(heads, near, parts, lanes, parts, lanes)
    two_front = behind(ahead(two, 2, me, parts), 4, me, parts)
    two_back = ahead(behind(two, 2, me, parts), 4, me, parts)
    two_front = two_front.transpose(1, 2, 0, 3, 4, 5).reshape(near, parts * rows, parts * lanes)
    two_back = two_back.transpose(1, 4, 0, 5, 2, 3).reshape(near, parts * rows, parts * lanes)
    matrix_two = widen(two_front, lanes, heads, lanes)
    matrix_two_back = widen(two_back, lanes, heads, lanes)

    three = level_three.reshape(heads, lanes, thirds, parts, near)
    three_front = behind(three, 3, me, parts).reshape(level_three.shape)
    three_back = ahead(three, 3, me, parts).reshape(level_three.shape)
    three_front = three_front.transpose(0, 2, 1, 3).reshape(heads, thirds * lanes, thirds)
    three_back = three_back.transpose(0, 3, 1, 2).reshape(heads, thirds * lanes, thirds)
    matrix_three = widen(three_front, 1, lanes, 1)
    matrix_three_back = widen(three_back, 1, lanes, 1)

    turned = tokens.transpose(2, 0, 1, 3)
    turned_up = upstream.transpose(2, 0, 1, 3)
    turned_rms = inverse_rms.transpose(2, 0, 1, 3)
    token_rows = normalised(turned, turned_rms, norm_gain).reshape(-1, channels)

    def half(values, n):
        return lax.dynamic_slice_in_dim(values, n * near, near, axis=0)

    outputs, gate_grads, normed_grads = [], [], []
    total_one = total_two = total_three = 0.0
    for n in range(CHUNKS):
        at = slice(n * width, (n + 1) * width)
        mixed = across_first(first_level(matrix_one, spreads[n]))
        mixed = mixed.reshape(thirds, rows, width)
        spread_two = exchange([half(mixed, (me + r) % parts) for r in range(parts)])
        second = exchange(list(second_level(matrix_two, spread_two)))
        second = [piece.reshape(near, heads, lanes, width) for piece in second]
        gate_pre = dot(token_rows, weight[:, at]).reshape(thirds, heads, lanes, width)
        output, gate_grad, grads, total = third_level(
            matrix_three, matrix_three_back, gate_pre, turned, turned_up, n, second
        )
        outputs.append(output)
        gate_grads.append(gate_grad)
        total_three = total_three + total
        grads = exchange([grad.reshape(near, rows, width) for grad in grads])
        grads, total = second_back(matrix_two_back, grads, spread_two, lanes, heads)
        total_two = total_two + total
        pieces = exchange(list(grads))
        joined = jnp.zeros((thirds, rows, width), BF16)
        for r in range(parts):
            place = ((me - r) % parts) * near
            joined = lax.dynamic_update_slice_in_dim(joined, pieces[r], place, axis=0)
        grads = across_first(joined.reshape(away, low, rows, width))
        grads, total = first_back(matrix_one_back, spreads[n], grads, lanes)
        total_one = total_one + total
        normed_grads.append(across_first(grads).reshape(thirds * rows, width))

    output = jnp.concatenate(outputs, axis=3).transpose(1, 2, 0, 3)
    grad_rows = jnp.concatenate(gate_grads, axis=3).reshape(-1, channels)
    back_term = jnp.einsum("tc,rc->tr", grad_rows, weight, preferred_element_type=F32)
    grad_hidden = jnp.concatenate(normed_grads, axis=1).astype(F32) + back_term
    weighted = grad_hidden.reshape(turned.shape) * norm_gain
    turned_float = turned.astype(F32)
    average = jnp.mean(weighted * turned_float, axis=3, keepdims=True)
    grad_tokens = (
        turned_up.astype(F32) + turned_rms * weighted - turned_float * turned_rms**3 * average
    ).astype(BF16)
    grad_tokens = grad_tokens.transpose(1, 2, 0, 3)

    scale = channels ** (-0.5)
    grad_one = total_one.reshape(low, firsts, lanes, firsts).transpose(2, 0, 1, 3) * scale
    grad_two = total_two.reshape(near, parts, heads, lanes, parts, lanes)
    grad_two = behind(behind(grad_two, 1, me, parts), 4, me, parts)
    grad_two = grad_two.transpose(2, 0, 1, 3, 4, 5).reshape(level_two.shape) * scale
    grad_three = total_three.reshape(heads, thirds, lanes, parts, near)
    grad_three = behind(grad_three, 3, me, parts).reshape(heads, thirds, lanes, thirds)
    grad_three = grad_three.transpose(0, 2, 1, 3) * scale
    return (output, grad_tokens, grad_one, grad_two, grad_three)


def solution(mesh):
    in_specs = (
        P("sa", "sb", None, None),
        P(),
        P(("sa", "sb"), None),
        P("sb", "sa", None, None),
        P("sa", "sb", None, None),
        P("sa", "sb", None, None),
        P("sa", "sb", None, None),
    )
    out_specs = (
        P("sa", "sb", None, None),
        P("sa", "sb", None, None),
        P("sb", "sa", None, None),
        P("sa", "sb", None, None),
        P("sa", "sb", None, None),
    )
    return jax.shard_map(
        functools.partial(body, mesh.shape["sb"], mesh.shape["sa"]),
        mesh=mesh,
        in_specs=in_specs,
        out_specs=out_specs,
        check_vma=False,
    )
```

```python
import functools
import math

import jax
import jax.numpy as jnp
from jax import lax
from jax.experimental import pallas as pl
from jax.experimental.pallas import tpu as pltpu
from jax.sharding import PartitionSpec as P


EPSILON = 1e-06
F32 = jnp.float32
BF16 = jnp.bfloat16
CHUNKS = 4
GROUPS = (1, 1, 2)
LIMIT = 60 * 1024 * 1024


def dot(left, right):
    return jnp.dot(left, right, preferred_element_type=F32)


def dot_last(left, right):
    return lax.dot_general(left, right, (((1,), (1,)), ((), ())), preferred_element_type=F32)


def position(shape, axis, inner, extent):
    return (lax.broadcasted_iota(jnp.int32, shape, axis) // inner) % extent


def widen(rows, inner, extent, lanes):
    _, count, width = rows.shape
    wide = width * extent
    source = lax.broadcasted_iota(jnp.int32, (width, wide), 0)
    column = lax.broadcasted_iota(jnp.int32, (width, wide), 1)
    pick = (source == (column // (extent * lanes)) * lanes + column % lanes).astype(BF16)
    full = jnp.einsum("brq,qw->brw", rows, pick, preferred_element_type=F32)
    keep = position((count, wide), 0, inner, extent) == position((count, wide), 1, lanes, extent)
    return jnp.where(keep[None], full, 0.0).astype(BF16)


def fold(total, inner, extent, lanes):
    count, wide = total.shape
    width = wide // extent
    keep = position((count, wide), 0, inner, extent) == position((count, wide), 1, lanes, extent)
    source = lax.broadcasted_iota(jnp.int32, (wide, width), 1)
    column = lax.broadcasted_iota(jnp.int32, (wide, width), 0)
    pick = (source == (column // (extent * lanes)) * lanes + column % lanes).astype(F32)
    return jnp.dot(
        jnp.where(keep, total, 0.0), pick, precision=lax.Precision.HIGHEST, preferred_element_type=F32
    )


def params(count):
    return pltpu.CompilerParams(
        dimension_semantics=("arbitrary",) * count, vmem_limit_bytes=LIMIT
    )


def cost(flops, moved):
    return pl.CostEstimate(flops=int(flops), bytes_accessed=int(moved), transcendentals=0)


def put(held, start, values):
    for tile in range(held.shape[0]):
        held[tile, start : start + values.shape[0], :] = values[:, tile * 128 : (tile + 1) * 128]


def take(held, start, count, stride):
    tiles = [held[tile, pl.ds(start, count, stride=stride), :] for tile in range(held.shape[0])]
    return jnp.concatenate(tiles, axis=-1)


def held_rows(rows, channels):
    return [pltpu.VMEM((channels // 128, rows, 128), F32)]


def first_kernel(matrix, values, out):
    shape = out.shape
    flat = values[...].reshape(-1, shape[3])
    out[...] = dot(matrix[0], flat).astype(BF16).reshape(shape)


def first_level(matrix, values, offset, width):
    away, low, rows, _ = values.shape
    if rows % 16:
        values = lax.slice_in_dim(values, offset * width, (offset + 1) * width, axis=3)
        flat = values.transpose(1, 0, 2, 3).reshape(low, away * rows, width)
        mixed = jnp.einsum("krs,ksc->krc", matrix, flat, preferred_element_type=F32).astype(BF16)
        return mixed.reshape(low, away, rows, width).transpose(1, 0, 2, 3)
    size = away * rows
    tile = min(width, 256)
    start = offset * (width // tile)
    spec = pl.BlockSpec((away, 1, rows, tile), lambda k, c: (0, k, 0, c + start))
    return pl.pallas_call(
        first_kernel,
        grid=(low, width // tile),
        in_specs=[pl.BlockSpec((1, size, size), lambda k, c: (k, 0, 0)), spec],
        out_specs=pl.BlockSpec((away, 1, rows, tile), lambda k, c: (0, k, 0, c)),
        out_shape=jax.ShapeDtypeStruct((away, low, rows, width), BF16),
        compiler_params=params(2),
        cost_estimate=cost(
            2 * low * size * size * width, 4 * low * size * width + 2 * matrix.size
        ),
        name="first",
    )(matrix, values)


def first_grad_kernel(lanes, values, grads, total):
    width = values.shape[3]
    flat = values[...].reshape(-1, width)
    grad = grads[...].reshape(-1, width)
    total[0] = fold(dot_last(grad, flat), 1, lanes, 1)


def first_grad(values, offset, grads, lanes):
    away, low, rows, width = grads.shape
    size = away * rows
    if rows % 16:
        values = lax.slice_in_dim(values, offset * width, (offset + 1) * width, axis=3)
        flat = values.transpose(1, 0, 2, 3).reshape(low, size, width)
        grad = grads.transpose(1, 0, 2, 3).reshape(low, size, width)
        full = jnp.einsum("krc,ksc->krs", grad, flat, preferred_element_type=F32)
        return jnp.stack([fold(full[k], 1, lanes, 1) for k in range(low)])
    halves = 2 if away % 2 == 0 else 1
    return pl.pallas_call(
        functools.partial(first_grad_kernel, lanes),
        grid=(low, halves),
        in_specs=[
            pl.BlockSpec((away, 1, rows, width), lambda k, h: (0, k, 0, offset)),
            pl.BlockSpec((away // halves, 1, rows, width), lambda k, h: (h, k, 0, 0)),
        ],
        out_specs=pl.BlockSpec((1, size // halves, size // lanes), lambda k, h: (k, h, 0)),
        out_shape=jax.ShapeDtypeStruct((low, size, size // lanes), F32),
        compiler_params=params(2),
        cost_estimate=cost(2 * low * size * size * width, 4 * grads.size),
        name="first_grad",
    )(values, grads)


def second_kernel(parts, matrix, *refs):
    ins, outs = refs[:parts], refs[parts:]
    rows = outs[0].shape[1]
    for k in range(matrix.shape[0]):
        flat = jnp.concatenate([ref[k] for ref in ins], axis=0)
        mixed = dot(matrix[k], flat).astype(BF16)
        for part in range(parts):
            outs[part][k] = mixed[part * rows : (part + 1) * rows]


def second_level(matrix, pieces):
    parts = len(pieces)
    count, rows, width = pieces[0].shape
    if rows % 16:
        flat = jnp.concatenate(pieces, axis=1)
        mixed = jnp.einsum("krs,ksc->krc", matrix, flat, preferred_element_type=F32).astype(BF16)
        return tuple(jnp.split(mixed, parts, axis=1))
    step = 4 if count % 4 == 0 else 1
    size = parts * rows
    spec = pl.BlockSpec((step, rows, width), lambda k: (k, 0, 0))
    return pl.pallas_call(
        functools.partial(second_kernel, parts),
        grid=(count // step,),
        in_specs=[pl.BlockSpec((step, size, size), lambda k: (k, 0, 0))] + [spec] * parts,
        out_specs=(spec,) * parts,
        out_shape=(jax.ShapeDtypeStruct(pieces[0].shape, BF16),) * parts,
        compiler_params=params(1),
        cost_estimate=cost(2 * count * size * size * width, 4 * parts * pieces[0].size),
        name="second",
    )(matrix, *pieces)


def second_back_kernel(parts, inner, lanes, matrix, *refs):
    grads, values = refs[:parts], refs[parts : 2 * parts]
    outs, total = refs[2 * parts : 3 * parts], refs[3 * parts]
    rows = outs[0].shape[1]
    for k in range(matrix.shape[0]):
        grad = jnp.concatenate([ref[k] for ref in grads], axis=0)
        flat = jnp.concatenate([ref[k] for ref in values], axis=0)
        mixed = dot(matrix[k], grad).astype(BF16)
        for part in range(parts):
            outs[part][k] = mixed[part * rows : (part + 1) * rows]
        total[k] = fold(dot_last(grad, flat), inner, lanes, inner)


def second_back(matrix, grads, values, inner, lanes):
    parts = len(grads)
    count, rows, width = grads[0].shape
    size = parts * rows
    if rows % 16:
        grad = jnp.concatenate(grads, axis=1)
        flat = jnp.concatenate(values, axis=1)
        mixed = jnp.einsum("krs,ksc->krc", matrix, grad, preferred_element_type=F32).astype(BF16)
        full = jnp.einsum("krc,ksc->krs", grad, flat, preferred_element_type=F32)
        total = jnp.stack([fold(full[k], inner, lanes, inner) for k in range(count)])
        return (tuple(jnp.split(mixed, parts, axis=1)), total)
    step = 4 if count % 4 == 0 else 1
    spec = pl.BlockSpec((step, rows, width), lambda k: (k, 0, 0))
    result = pl.pallas_call(
        functools.partial(second_back_kernel, parts, inner, lanes),
        grid=(count // step,),
        in_specs=[pl.BlockSpec((step, size, size), lambda k: (k, 0, 0))] + [spec] * (2 * parts),
        out_specs=(spec,) * parts
        + (pl.BlockSpec((step, size, size // lanes), lambda k: (k, 0, 0)),),
        out_shape=(jax.ShapeDtypeStruct(grads[0].shape, BF16),) * parts
        + (jax.ShapeDtypeStruct((count, size, size // lanes), F32),),
        compiler_params=params(1),
        cost_estimate=cost(4 * count * size * size * width, 6 * parts * grads[0].size),
        name="second_back",
    )(matrix, *grads, *values)
    return (result[:parts], result[parts])


def gate_math(mixed, gate_pre, tokens, upstream):
    gate_sigmoid = jax.nn.sigmoid(gate_pre)
    gate_value = gate_pre * gate_sigmoid
    output = tokens.astype(F32) + mixed * gate_value
    upstream = upstream.astype(F32)
    grad_mixed = (upstream * gate_value).astype(BF16)
    grad_gate = (
        upstream * mixed * gate_sigmoid * (1.0 + gate_pre * (1.0 - gate_sigmoid))
    ).astype(BF16)
    return (output, grad_mixed, grad_gate)


def third_kernel(parts, lanes, kept, matrix, matrix_back, gate_pre, tokens, upstream, *refs):
    ins = refs[:parts]
    output, grad_gate = refs[parts + kept : parts + kept + 2]
    outs, total = refs[parts + kept + 2 : 2 * parts + kept + 2], refs[2 * parts + kept + 2]
    held = refs[2 * parts + kept + 3]
    shape = grad_gate.shape
    width = shape[3]
    flat = jnp.concatenate([ref[...].reshape(-1, width) for ref in ins], axis=0)
    mixed = dot(matrix[0], flat)
    result, grad_mixed, gate_grad = gate_math(
        mixed,
        gate_pre[...].reshape(-1, width),
        tokens[...].reshape(-1, width),
        upstream[...].reshape(-1, width),
    )
    put(held, 0, result)
    for lane in range(lanes):
        output[0, lane] = take(held, lane, shape[0], lanes).astype(BF16)
    grad_gate[...] = gate_grad.reshape(shape)
    back = dot(matrix_back[0], grad_mixed).astype(BF16)
    rows = back.shape[0] // parts
    for part in range(parts):
        outs[part][...] = back[part * rows : (part + 1) * rows].reshape(outs[part].shape)
    total[0] = fold(dot_last(grad_mixed, flat), 1, lanes, 1)


def third_level(matrix, matrix_back, gate_pre, tokens, upstream, offset, pieces, kept):
    parts = len(pieces)
    low, heads, lanes, width = pieces[0].shape
    count = low * parts
    size = count * lanes
    if lanes % 16:
        flat = jnp.concatenate(pieces, axis=0).transpose(1, 0, 2, 3).reshape(heads, size, width)
        mixed = jnp.einsum("irs,isc->irc", matrix, flat, preferred_element_type=F32)

        def turn_back(value):
            return value.reshape(heads, count, lanes, width).transpose(1, 0, 2, 3)

        def local(value):
            value = lax.slice_in_dim(value, offset * width, (offset + 1) * width, axis=3)
            return value.transpose(1, 0, 2, 3).reshape(heads, size, width)

        pre = gate_pre.transpose(1, 0, 2, 3).reshape(heads, size, width)
        result, grad_mixed, gate_grad = gate_math(mixed, pre, local(tokens), local(upstream))
        back = jnp.einsum("irs,isc->irc", matrix_back, grad_mixed, preferred_element_type=F32)
        full = jnp.einsum("irc,isc->irs", grad_mixed, flat, preferred_element_type=F32)
        total = jnp.stack([fold(full[i], 1, lanes, 1) for i in range(heads)])
        outs = tuple(jnp.split(turn_back(back.astype(BF16)), parts, axis=0))
        result = turn_back(result).astype(BF16).transpose(1, 2, 0, 3)
        gate_grad = turn_back(gate_grad)
        if kept:
            result = jnp.concatenate([kept[0], result], axis=3)
            gate_grad = jnp.concatenate([kept[1], gate_grad], axis=3)
        return (result, gate_grad, outs, total)
    channels = tokens.shape[3]
    whole = pl.BlockSpec((count, 1, lanes, width), lambda i: (0, i, 0, 0))
    shifted = pl.BlockSpec((count, 1, lanes, width), lambda i: (0, i, 0, offset))
    natural = pl.BlockSpec((1, lanes, count, width), lambda i: (i, 0, 0, offset))
    part = pl.BlockSpec((low, 1, lanes, width), lambda i: (0, i, 0, 0))
    square = pl.BlockSpec((1, size, size), lambda i: (i, 0, 0))
    first = 5 + parts
    result = pl.pallas_call(
        functools.partial(third_kernel, parts, lanes, len(kept)),
        grid=(heads,),
        in_specs=[square, square, whole, shifted, shifted]
        + [part] * parts
        + [pl.BlockSpec(memory_space=pl.ANY)] * len(kept),
        out_specs=(natural, shifted)
        + (part,) * parts
        + (pl.BlockSpec((1, size, count), lambda i: (i, 0, 0)),),
        out_shape=(
            jax.ShapeDtypeStruct((heads, lanes, count, channels), BF16),
            jax.ShapeDtypeStruct((count, heads, lanes, channels), BF16),
        )
        + (jax.ShapeDtypeStruct(pieces[0].shape, BF16),) * parts
        + (jax.ShapeDtypeStruct((heads, size, count), F32),),
        scratch_shapes=held_rows(size, width),
        input_output_aliases={first + n: n for n in range(len(kept))},
        compiler_params=params(1),
        cost_estimate=cost(6 * heads * size * size * width, 18 * heads * size * width),
        name="third",
    )(matrix, matrix_back, gate_pre, tokens, upstream, *pieces, *kept)
    return (result[0], result[1], result[2 : parts + 2], result[parts + 2])


def enter_math(values, gain):
    scale = lax.rsqrt(jnp.mean(values * values, axis=-1, keepdims=True) + EPSILON)
    return (values * scale * gain).astype(BF16)


def head_kernel(tokens, gain, chunk, held):
    values = tokens[0].astype(F32)
    width = chunk.shape[3]
    scale = lax.rsqrt(jnp.mean(values * values, axis=-1, keepdims=True) + EPSILON)
    result = values[..., :width] * scale * gain[:, :width].reshape(1, 1, width)
    put(held, 0, result.reshape(-1, width))
    step, lanes = chunk.shape[0], chunk.shape[2]
    for k in range(step):
        chunk[k, 0] = take(held, k, lanes, step).astype(BF16)


def enter_kernel(tokens, gain, turned, normed, *refs):
    chunks, held = refs[:-1], refs[-1]
    step, lanes = turned.shape[0], turned.shape[2]
    put(held, 0, tokens[0].astype(F32).reshape(lanes * step, -1))
    for k in range(step):
        values = take(held, k, lanes, step)
        result = enter_math(values, gain[...])
        turned[k, 0] = values.astype(BF16)
        normed[k, 0] = result
        stop = result.shape[1]
        for chunk in reversed(chunks):
            chunk[k, 0] = result[:, stop - chunk.shape[3] : stop]
            stop -= chunk.shape[3]


def turn_kernel(values, turned, held):
    step, lanes = turned.shape[0], turned.shape[2]
    put(held, 0, values[0].astype(F32).reshape(lanes * step, -1))
    for k in range(step):
        turned[k, 0] = take(held, k, lanes, step).astype(BF16)


STEP = 16


def natural_spec(lanes, channels):
    return pl.BlockSpec((1, lanes, STEP, channels), lambda i, k: (i, 0, k, 0))


def turned_spec(lanes, channels):
    return pl.BlockSpec((STEP, 1, lanes, channels), lambda i, k: (k, i, 0, 0))


def head(tokens, gain):
    heads, lanes, count, channels = tokens.shape
    width = channels // CHUNKS
    if lanes % 16 or count % STEP:
        return enter_math(tokens.transpose(2, 0, 1, 3).astype(F32), gain)[..., :width]
    return pl.pallas_call(
        head_kernel,
        grid=(heads, count // STEP),
        in_specs=[natural_spec(lanes, channels), pl.BlockSpec((1, channels), lambda i, k: (0, 0))],
        out_specs=turned_spec(lanes, width),
        out_shape=jax.ShapeDtypeStruct((count, heads, lanes, width), BF16),
        scratch_shapes=held_rows(lanes * STEP, width),
        compiler_params=params(2),
        cost_estimate=cost(4 * tokens.size, 3 * tokens.size),
        name="head",
    )(tokens, gain.reshape(1, channels))


def enter(tokens, gain):
    heads, lanes, count, channels = tokens.shape
    width = channels // CHUNKS
    if lanes % 16 or count % STEP:
        turned = tokens.transpose(2, 0, 1, 3)
        normed = enter_math(turned.astype(F32), gain)
        edges = [sum(GROUPS[: n + 1]) * width for n in range(len(GROUPS) - 1)]
        return (turned, normed) + tuple(jnp.split(normed, edges, axis=3)[1:])
    full = jax.ShapeDtypeStruct((count, heads, lanes, channels), BF16)
    widths = [group * width for group in GROUPS[1:]]
    return pl.pallas_call(
        enter_kernel,
        grid=(heads, count // STEP),
        in_specs=[natural_spec(lanes, channels), pl.BlockSpec((1, channels), lambda i, k: (0, 0))],
        out_specs=(turned_spec(lanes, channels),) * 2
        + tuple(turned_spec(lanes, part) for part in widths),
        out_shape=(full, full)
        + tuple(jax.ShapeDtypeStruct((count, heads, lanes, part), BF16) for part in widths),
        scratch_shapes=held_rows(lanes * STEP, channels),
        compiler_params=params(2),
        cost_estimate=cost(8 * tokens.size, 8 * tokens.size),
        name="enter",
    )(tokens, gain.reshape(1, channels))


def turn(values):
    heads, lanes, count, channels = values.shape
    if lanes % 16 or count % STEP:
        return values.transpose(2, 0, 1, 3)
    return pl.pallas_call(
        turn_kernel,
        grid=(heads, count // STEP),
        in_specs=[natural_spec(lanes, channels)],
        out_specs=turned_spec(lanes, channels),
        out_shape=jax.ShapeDtypeStruct((count, heads, lanes, channels), BF16),
        scratch_shapes=held_rows(lanes * STEP, channels),
        compiler_params=params(2),
        cost_estimate=cost(values.size, 4 * values.size),
        name="turn",
    )(values)


def last_math(grads, back, tokens, upstream, gain):
    tokens = tokens.astype(F32)
    scale = lax.rsqrt(jnp.mean(tokens * tokens, axis=-1, keepdims=True) + EPSILON)
    weighted = (grads.astype(F32) + back.astype(F32)) * gain
    average = jnp.mean(weighted * tokens, axis=-1, keepdims=True)
    return upstream.astype(F32) + scale * weighted - tokens * (scale**3 * average)


def last_kernel(back, tokens, upstream, gain, *refs):
    grads, out, held = refs[:-2], refs[-2], refs[-1]
    step, lanes = back.shape[0], back.shape[2]
    for k in range(step):
        grad = jnp.concatenate([ref[k, 0] for ref in grads], axis=-1)
        result = last_math(grad, back[k, 0], tokens[k, 0], upstream[k, 0], gain[...])
        put(held, k * lanes, result)
    for lane in range(lanes):
        out[0, lane] = take(held, lane, step, lanes).astype(BF16)


def last(grads, back, tokens, upstream, gain):
    count, heads, lanes, channels = tokens.shape
    if lanes % 16 or count % STEP:
        result = last_math(jnp.concatenate(grads, axis=3), back, tokens, upstream, gain)
        return result.astype(BF16).transpose(1, 2, 0, 3)
    whole = turned_spec(lanes, channels)
    return pl.pallas_call(
        last_kernel,
        grid=(heads, count // STEP),
        in_specs=[whole, whole, whole, pl.BlockSpec((1, channels), lambda i, k: (0, 0))]
        + [turned_spec(lanes, grads[0].shape[3])] * len(grads),
        out_specs=natural_spec(lanes, channels),
        out_shape=jax.ShapeDtypeStruct((heads, lanes, count, channels), BF16),
        scratch_shapes=held_rows(lanes * STEP, channels),
        compiler_params=params(2),
        cost_estimate=cost(10 * tokens.size, 12 * tokens.size),
        name="last",
    )(back, tokens, upstream, gain.reshape(1, channels), *grads)


def reorder(blocks, me, sign):
    count = len(blocks)
    result = []
    for r in range(count):
        block = blocks[0]
        for n in range(1, count):
            block = jnp.where((me + sign * r) % count == n, blocks[n], block)
        result.append(block)
    return result


def reorder_along(values, axis, me, sign):
    blocks = [lax.index_in_dim(values, n, axis, keepdims=False) for n in range(values.shape[axis])]
    return jnp.stack(reorder(blocks, me, sign), axis=axis)


def exchange(blocks):
    count = len(blocks)
    return [blocks[0]] + [
        lax.ppermute(blocks[r], "sb", [(n, (n + r) % count) for n in range(count)])
        for r in range(1, count)
    ]


def pair_kernel(flag, own, other, out):
    upper = flag[0] == 1
    out[0, 0] = jnp.where(upper, other[0], own[0])
    out[0, 1] = jnp.where(upper, own[0], other[0])


def pair(upper, own, other, place):
    lead, rest, channels = own.shape[:place], own.shape[place:-1], own.shape[-1]
    count, rows = math.prod(lead), math.prod(rest)
    if rows % 16:
        ordered = [jnp.where(upper, other, own), jnp.where(upper, own, other)]
        return jnp.stack(ordered, axis=place)
    spec = pl.BlockSpec((1, rows, channels), lambda n, flag: (n, 0, 0))
    result = pl.pallas_call(
        pair_kernel,
        grid_spec=pltpu.PrefetchScalarGridSpec(
            num_scalar_prefetch=1,
            grid=(count,),
            in_specs=[spec, spec],
            out_specs=pl.BlockSpec((1, 2, rows, channels), lambda n, flag: (n, 0, 0, 0)),
        ),
        out_shape=jax.ShapeDtypeStruct((count, 2, rows, channels), BF16),
        compiler_params=params(1),
        cost_estimate=cost(own.size, 8 * own.size),
        name="pair",
    )(
        upper.astype(jnp.int32).reshape(1),
        own.reshape(count, rows, channels),
        other.reshape(count, rows, channels),
    )
    return result.reshape(lead + (2,) + rest + (channels,))


def gather_rows(rows, away, parts, me):
    spot = lax.axis_index("sa")
    bits = away.bit_length() - 1
    if away != 1 << bits:
        return lax.all_gather(rows, ("sa", "sb"), axis=0, tiled=True)

    def double(rows, place):
        bit = 1 << (bits - 1 - place)
        other = lax.ppermute(rows, "sa", [(n, n ^ bit) for n in range(away)])
        upper = (spot // bit) % 2 == 1
        return pair(upper, rows, other, place)

    for place in range(bits):
        if place == min(2, bits - 1):
            blocks = exchange([rows] * parts)
            rows = jnp.stack(reorder(blocks, me, -1), axis=place)
        rows = double(rows, place)
    return rows


def across_first(values):
    return lax.all_to_all(values, "sa", split_axis=0, concat_axis=0, tiled=True)


def body(parts, away, tokens, norm_gain, gate_weight, level_one, level_two, level_three, upstream):
    heads, lanes, thirds, channels = tokens.shape
    firsts = level_one.shape[2]
    low = thirds // away
    near = thirds // parts
    me = lax.axis_index("sb")
    width = channels // CHUNKS
    rows = heads * lanes

    weight = gather_rows(gate_weight, away, parts, me).reshape(-1, channels)

    turned, normed, *chunks = enter(tokens, norm_gain)
    chunks = [head(tokens, norm_gain)] + chunks
    token_rows = normed.reshape(-1, channels)
    spreads = []
    for n, group in enumerate(GROUPS):
        spread = across_first(chunks[n].reshape(away, low, rows, group * width))
        spreads += [(spread, offset) for offset in range(group)]
    turned_up = turn(upstream)

    one = level_one.transpose(1, 2, 0, 3).reshape(low, firsts * lanes, firsts)
    one_back = level_one.transpose(1, 3, 0, 2).reshape(low, firsts * lanes, firsts)
    matrix_one = widen(one, 1, lanes, 1)
    matrix_one_back = widen(one_back, 1, lanes, 1)

    two = level_two.reshape(heads, near, parts, lanes, parts, lanes)
    two_front = reorder_along(reorder_along(two, 2, me, 1), 4, me, -1)
    two_back = reorder_along(reorder_along(two, 2, me, -1), 4, me, 1)
    two_front = two_front.transpose(1, 2, 0, 3, 4, 5).reshape(near, parts * rows, parts * lanes)
    two_back = two_back.transpose(1, 4, 0, 5, 2, 3).reshape(near, parts * rows, parts * lanes)
    matrix_two = widen(two_front, lanes, heads, lanes)
    matrix_two_back = widen(two_back, lanes, heads, lanes)

    three = level_three.reshape(heads, lanes, thirds, parts, near)
    three_front = reorder_along(three, 3, me, -1).reshape(level_three.shape)
    three_back = reorder_along(three, 3, me, 1).reshape(level_three.shape)
    three_front = three_front.transpose(0, 2, 1, 3).reshape(heads, thirds * lanes, thirds)
    three_back = three_back.transpose(0, 3, 1, 2).reshape(heads, thirds * lanes, thirds)
    matrix_three = widen(three_front, 1, lanes, 1)
    matrix_three_back = widen(three_back, 1, lanes, 1)

    def half(values, n):
        return lax.dynamic_slice_in_dim(values, n * near, near, axis=0)

    kept, normed_grads = (), []
    total_one = total_two = total_three = 0.0
    for n in range(CHUNKS):
        at = slice(n * width, (n + 1) * width)
        mixed = first_level(matrix_one, *spreads[n], width)
        mixed = across_first(mixed)
        mixed = mixed.reshape(thirds, rows, width)
        spread_two = [half(mixed, (me + r) % parts) for r in range(parts)]
        spread_two = exchange(spread_two)
        second = second_level(matrix_two, spread_two)
        second = exchange(list(second))
        second = [piece.reshape(near, heads, lanes, width) for piece in second]
        gate_pre = dot(token_rows, weight[:, at]).reshape(thirds, heads, lanes, width)
        output, gate_grad, grads, total = third_level(
            matrix_three, matrix_three_back, gate_pre, turned, turned_up, n, second, kept
        )
        kept = (output, gate_grad)
        total_three = total_three + total
        grads = [grad.reshape(near, rows, width) for grad in grads]
        grads = exchange(grads)
        grads, total = second_back(matrix_two_back, grads, spread_two, lanes, heads)
        total_two = total_two + total
        pieces = exchange(list(grads))
        joined = jnp.concatenate(reorder(pieces, me, -1), axis=0)
        grads = across_first(joined.reshape(away, low, rows, width))
        back = first_level(matrix_one_back, grads, 0, width)
        back = across_first(back)
        total_one = total_one + first_grad(*spreads[n], grads, lanes)
        normed_grads.append(back.reshape(thirds, heads, lanes, width))

    grad_rows = gate_grad.reshape(-1, channels)
    back_term = jnp.einsum("tc,rc->tr", grad_rows, weight, preferred_element_type=F32)
    back_term = back_term.astype(BF16)
    grad_tokens = last(normed_grads, back_term.reshape(turned.shape), turned, turned_up, norm_gain)

    scale = channels ** (-0.5)
    grad_one = total_one.reshape(low, firsts, lanes, firsts).transpose(2, 0, 1, 3) * scale
    grad_two = total_two.reshape(near, parts, heads, lanes, parts, lanes)
    grad_two = reorder_along(reorder_along(grad_two, 1, me, -1), 4, me, -1)
    grad_two = grad_two.transpose(2, 0, 1, 3, 4, 5).reshape(level_two.shape) * scale
    grad_three = total_three.reshape(heads, thirds, lanes, parts, near)
    grad_three = reorder_along(grad_three, 3, me, -1).reshape(heads, thirds, lanes, thirds)
    grad_three = grad_three.transpose(0, 2, 1, 3) * scale
    return (output, grad_tokens, grad_one, grad_two, grad_three)


def solution(mesh):
    in_specs = (
        P("sa", "sb", None, None),
        P(),
        P(("sa", "sb"), None),
        P("sb", "sa", None, None),
        P("sa", "sb", None, None),
        P("sa", "sb", None, None),
        P("sa", "sb", None, None),
    )
    out_specs = (
        P("sa", "sb", None, None),
        P("sa", "sb", None, None),
        P("sb", "sa", None, None),
        P("sa", "sb", None, None),
        P("sa", "sb", None, None),
    )
    return jax.shard_map(
        functools.partial(body, mesh.shape["sb"], mesh.shape["sa"]),
        mesh=mesh,
        in_specs=in_specs,
        out_specs=out_specs,
        check_vma=False,
    )
```
